32 devices in a mesh: row: 4 (over x, core), vec: 8 (over z, y).
Axes of the slice: x: 2, y: 2, z: 4, core: 2. Of those that a mesh axis runs over, the one named last changes fastest.
Arguments:
- old_vectors: float32 [640, 12288], P('vec', 'row'), may hold values from -6 to 6
- panel_source: int32 [256], replicated, may hold values from 0 to 639, as said below
- secular: float32 [1024, 256], P('vec'), may hold values from -0.375 to 0.375
- reflectors: float32 [256, 12288], P('vec', 'row'), may hold values from -6 to 6
- wy_factor: float32 [256, 256], replicated, as said below
- cholesky_panel: float32 [256, 12288], P('vec', 'row'), may hold values from -0.0546875 to 0.0546875
- panel_inverse: float32 [256, 256], replicated, as said below
Outputs:
- vectors: float32 [1024, 12288], P('vec', 'row')
The draws below stay inside these ranges and needn't reach their ends.
Inputs may be any that keep to these rules, and one draw needn't show every extreme that they name: `panel_source`: distinct numbers; each block of 80 consecutive old vectors (those of one index of vec) supplies at most 48 panel columns, and some block supplies exactly 48. `wy_factor`: upper triangular. `panel_inverse`: upper triangular.
All inputs are finite; a program needn't handle non-finite values.
Results may differ from the reference program's by a relative error of at most 0.0001.
Values sent between devices are 32-bit elements; how exact they have to be, the bound alone decides.
A program may use at most 64 MiB of HBM per device.

```python
import jax
import jax.numpy as jnp
from jax import lax

PANEL = 256
MAXC = 48
QV_DEV = 80
OLDV = 640
ORDER = 12288
VECTORS = 1024


def draw_panel_source(key, part):
    subkeys = jax.random.split(jax.random.fold_in(key, 11), 4)
    blocks = OLDV // QV_DEV
    scores = jax.random.randint(subkeys[0], (blocks, QV_DEV), 0, 1 << 30)
    local_pick = jnp.argsort(scores, axis=1, stable=True)[:, :MAXC].astype(jnp.int32)
    candidates = (local_pick + QV_DEV * jnp.arange(blocks, dtype=jnp.int32)[:, None]).reshape(-1)
    busiest = jax.random.randint(subkeys[1], (), 0, blocks)
    block_of = jnp.repeat(jnp.arange(blocks, dtype=jnp.int32), MAXC)
    priority = jax.random.randint(subkeys[2], (blocks * MAXC,), 0, 1 << 20) + jnp.where(block_of == busiest, 1 << 21, 0)
    ranking = jnp.argsort(-priority, stable=True)
    chosen = candidates[ranking[:PANEL]]
    return jax.random.permutation(subkeys[3], chosen).astype(jnp.int32)


def draw_wy_factor(key, part):
    subkeys = jax.random.split(jax.random.fold_in(key, 23), 2)
    diagonal = jax.random.uniform(subkeys[0], (PANEL,), jnp.float32, 1.0, 2.0)
    off_diagonal = jax.random.normal(subkeys[1], (PANEL, PANEL), jnp.float32) / jnp.sqrt(jnp.float32(PANEL))
    matrix = jnp.triu(off_diagonal, 1) + jnp.diag(diagonal)
    return 4.0 / ORDER * matrix


def draw_panel_inverse(key, part):
    subkeys = jax.random.split(jax.random.fold_in(key, 37), 2)
    diagonal = jnp.exp(jax.random.uniform(subkeys[0], (PANEL,), jnp.float32, -0.7, 0.7))
    off_diagonal = 0.6 * jax.random.normal(subkeys[1], (PANEL, PANEL), jnp.float32) / jnp.sqrt(jnp.float32(PANEL))
    return jnp.triu(off_diagonal, 1) + jnp.diag(diagonal)


def block_levels(stream_key, dims, shards, smallest, high):
    def one(axis_at, blocks):
        steps = jax.random.uniform(jax.random.fold_in(jax.random.fold_in(stream_key, 6), axis_at), (blocks,), jnp.float32, smallest / len(shards), high / len(shards))
        return jnp.repeat(jnp.exp(steps), dims[axis_at] // blocks).reshape((-1,) + (1,) * (len(dims) - axis_at - 1))

    factor_of = one(*shards[0])
    for cut in shards[1:]:
        factor_of = factor_of * one(*cut)
    return factor_of


def scatter_about(stream_key, shape, spread, most, shards=(), held_as=jnp.bfloat16):
    drawn = spread * jax.random.normal(stream_key, shape, jnp.float32)
    if shards:
        drawn = drawn * block_levels(stream_key, shape, shards, -0.22, 0.18)
    return jnp.clip(drawn, -most, most).astype(held_as)


def setup_inputs(seed: int = 0) -> dict:
    key_list = jax.random.split(jax.random.key(seed), 8)
    return {
        "old_vectors": scatter_about(key_list[0], (OLDV, ORDER), 1.0, 6.0, ((0, 8), (1, 4)), jnp.float32),
        "panel_source": draw_panel_source(jax.random.fold_in(key_list[7], 71), 0),
        "secular": scatter_about(key_list[2], (VECTORS, PANEL), PANEL ** -0.5, 0.375, ((0, 8),), jnp.float32),
        "reflectors": scatter_about(key_list[3], (PANEL, ORDER), 1.0, 6.0, ((0, 8), (1, 4)), jnp.float32),
        "wy_factor": draw_wy_factor(jax.random.fold_in(key_list[7], 71), 0),
        "cholesky_panel": scatter_about(key_list[5], (PANEL, ORDER), ORDER ** -0.5, 0.0546875, ((0, 8), (1, 4)), jnp.float32),
        "panel_inverse": draw_panel_inverse(jax.random.fold_in(key_list[7], 71), 0),
    }


def product(left, right):
    return jnp.dot(left, right, precision=lax.Precision.HIGHEST, preferred_element_type=jnp.float32)


def reference(old_vectors, panel_source, secular, reflectors, wy_factor, cholesky_panel, panel_inverse):
    picked = jnp.take(old_vectors, panel_source, axis=0)
    merged = product(secular, picked)
    inner_products = product(merged, reflectors.T)
    wy_coeff = product(inner_products, wy_factor.T)
    applied = merged - product(wy_coeff, reflectors)
    correction = product(applied[:, PANEL:], cholesky_panel[:, PANEL:].T)
    top_rows = product(applied[:, :PANEL] - correction, panel_inverse.T)
    return jnp.concatenate([top_rows, applied[:, PANEL:]], axis=1)
```

```python
import functools
import math

import jax
import jax.numpy as jnp
from jax import lax
from jax.experimental import pallas as pl
from jax.experimental.pallas import tpu as pltpu
from jax.sharding import PartitionSpec as P

MESH = pl.DeviceIdType.MESH


def product(left, right):
    return jnp.dot(left, right, precision=lax.Precision.HIGHEST, preferred_element_type=jnp.float32)


def product_t(left, right):
    return lax.dot_general(
        left,
        right,
        (((1,), (1,)), ((), ())),
        precision=lax.Precision.HIGHEST,
        preferred_element_type=jnp.float32,
    )


def kernel(
    nrow, zn, yn, slots,
    own_ref, chol_ref, slot_ref, secular_ref, wy_ref, pinv_ref,
    out_ref,
    kbuf, gram, rbuf, gall_y, gall_c, smap,
    own_sem, send_z, send_y, recv_k, send_r, recv_r, send_g, recv_g, send_c, recv_c,
):
    nvec = zn * yn
    rows, ncol = own_ref.shape
    refl = rows - slots
    panel = secular_ref.shape[1]
    r = lax.axis_index("row")
    v = lax.axis_index("vec")
    z = v // yn
    y = v % yn

    barrier = pltpu.get_barrier_semaphore()

    @pl.loop(1, nrow)
    def _(k):
        pl.semaphore_signal(barrier, inc=1, device_id=((r + k) % nrow, v), device_id_type=MESH)

    @pl.loop(1, nvec)
    def _(k):
        pl.semaphore_signal(barrier, inc=1, device_id=(r, (v + k) % nvec), device_id_type=MESH)

    pl.semaphore_wait(barrier, nrow - 1 + nvec - 1)

    def block_copy(src, block, target, send_sem):
        return pltpu.make_async_remote_copy(
            src_ref=src,
            dst_ref=kbuf.at[block],
            send_sem=send_sem,
            recv_sem=recv_k.at[block],
            device_id=(r, target),
            device_id_type=MESH,
        )

    def z_copy(src, block, sign):
        return block_copy(src, block, v + sign * yn, send_z.at[(sign + 1) // 2, block])

    def y_copy(src, block, sign):
        return block_copy(src, block, v + sign, send_y.at[(sign + 1) // 2, block])

    def z_ok(sign):
        return (z + sign >= 0) & (z + sign < zn)

    def y_ok(sign):
        return (y + sign >= 0) & (y + sign < yn)

    own_copy = pltpu.make_async_copy(own_ref, kbuf.at[v], own_sem)
    for sign in (-1, 1):

        @pl.when(z_ok(sign))
        def _():
            z_copy(own_ref, v, sign).start()

        @pl.when(y_ok(sign))
        def _():
            y_copy(own_ref, v, sign).start()

    own_copy.start()
    gram[...] = jnp.zeros_like(gram)
    row_iota = lax.broadcasted_iota(jnp.int32, (nvec * slots, panel), 0)
    every = jnp.where(row_iota == slot_ref[0:1, :], 1.0, 0.0).astype(jnp.float32)
    smap[...] = product_t(secular_ref[...], every)

    step = math.gcd(ncol, 768)

    def add_gram(block):
        def body(i, carry):
            with_y, with_c, y_with_c = carry
            cols = pl.ds(pl.multiple_of(i * step, step), step)
            picked = kbuf[block, 0:slots, cols]
            with_y = with_y + product_t(own_ref[slots:rows, cols], picked)
            masked = chol_ref[:, cols]
            with_c = with_c + product_t(masked, picked)
            y_with_c = y_with_c + product_t(masked, kbuf[block, slots:rows, cols])
            return with_y, with_c, y_with_c

        zero = jnp.zeros((refl, slots), jnp.float32)
        with_y, with_c, y_with_c = lax.fori_loop(
            0, ncol // step, body, (zero, zero, jnp.zeros((refl, refl), jnp.float32))
        )
        slot_iota = lax.broadcasted_iota(jnp.int32, (slots, panel), 0) + block * slots
        chosen = jnp.where(slot_iota == slot_ref[0:1, :], 1.0, 0.0).astype(jnp.float32)
        lane = lax.broadcasted_iota(jnp.int32, (refl, panel), 1)
        sub = lax.broadcasted_iota(jnp.int32, (refl, panel), 0) + block * refl
        placed = jnp.where(lane == sub, 1.0, 0.0).astype(jnp.float32)
        gram[0:refl] += product(with_y, chosen)
        gram[refl : 2 * refl] += product(with_c, chosen)
        gram[2 * refl : 3 * refl] += product(y_with_c, placed)

    own_copy.wait()
    add_gram(v)

    def wait_block(block):
        pltpu.make_async_remote_copy(
            src_ref=kbuf.at[block],
            dst_ref=kbuf.at[block],
            send_sem=own_sem,
            recv_sem=recv_k.at[block],
            device_id=(r, v),
            device_id_type=MESH,
        ).wait_recv()

    @pl.loop(1, zn + 1)
    def _(d):
        for side in (-1, 1):
            zz = z + side * d

            @pl.when((zz >= 0) & (zz < zn))
            def _():
                block = zz * yn + y
                wait_block(block)

                @pl.when(z_ok(-side))
                def _():
                    z_copy(kbuf.at[block], block, -side).start()

                for sign in (-1, 1):

                    @pl.when(y_ok(sign))
                    def _():
                        y_copy(kbuf.at[block], block, sign).start()

        for side in (-1, 1):
            zz = z + side * d

            @pl.when((zz >= 0) & (zz < zn))
            def _():
                add_gram(zz * yn + y)

        e = d - 1
        for side in (-1, 1):
            zz = z + side * e

            @pl.when((zz >= 0) & (zz < zn) & ((side < 0) | (e > 0)))
            def _():
                @pl.loop(1, yn)
                def _(h):
                    for sign in (-1, 1):
                        yy = y + sign * h

                        @pl.when((yy >= 0) & (yy < yn))
                        def _():
                            block = zz * yn + yy
                            wait_block(block)

                            @pl.when(y_ok(-sign))
                            def _():
                                y_copy(kbuf.at[block], block, -sign).start()

                            add_gram(block)

    rbuf[r] = gram[...]

    def row_copy(k):
        return pltpu.make_async_remote_copy(
            src_ref=gram,
            dst_ref=rbuf.at[r],
            send_sem=send_r.at[k],
            recv_sem=recv_r.at[r],
            device_id=((r + k) % nrow, v),
            device_id_type=MESH,
        )

    def row_arrival(k):
        return pltpu.make_async_remote_copy(
            src_ref=gram,
            dst_ref=rbuf.at[(r + k) % nrow],
            send_sem=send_r.at[k],
            recv_sem=recv_r.at[(r + k) % nrow],
            device_id=((r + k) % nrow, v),
            device_id_type=MESH,
        )

    @pl.loop(1, nrow)
    def _(k):
        row_copy(k).start()

    wide = math.gcd(ncol, 512)

    def merge(low, high):
        @pl.loop(low, high)
        def _(i):
            cols = pl.ds(pl.multiple_of(i * wide, wide), wide)
            picked = kbuf[:, 0:slots, cols].reshape(nvec * slots, wide)
            out_ref[:, cols] = product(smap[...], picked)

    half = (ncol // wide) // 2
    merge(0, half)

    @pl.loop(1, nrow)
    def _(k):
        row_arrival(k).wait_recv()

    total = rbuf[0]
    for k in range(1, nrow):
        total = total + rbuf[k]
    gall_y[v] = total[0:refl]
    gall_c[v] = total[refl:]

    def vec_copy(buf, send, recv, k, slot):
        return pltpu.make_async_remote_copy(
            src_ref=buf.at[v],
            dst_ref=buf.at[slot],
            send_sem=send.at[k],
            recv_sem=recv.at[slot],
            device_id=(r, (v + k) % nvec),
            device_id_type=MESH,
        )

    @pl.loop(1, nvec)
    def _(k):
        vec_copy(gall_y, send_g, recv_g, k, v).start()

    @pl.when(r == 0)
    def _():
        @pl.loop(1, nvec)
        def _(k):
            vec_copy(gall_c, send_c, recv_c, k, v).start()

    merge(half, ncol // wide)

    @pl.loop(1, nvec)
    def _(k):
        vec_copy(gall_y, send_g, recv_g, k, (v + k) % nvec).wait_recv()

    inner = product_t(secular_ref[...], gall_y[...].reshape(panel, panel))
    coeff = product_t(inner, wy_ref[...])

    @pl.loop(0, ncol // wide)
    def _(i):
        cols = pl.ds(pl.multiple_of(i * wide, wide), wide)
        householder = kbuf[:, slots:rows, cols].reshape(panel, wide)
        out_ref[:, cols] = out_ref[:, cols] - product(coeff, householder)

    @pl.when(r == 0)
    def _():
        @pl.loop(1, nvec)
        def _(k):
            vec_copy(gall_c, send_c, recv_c, k, (v + k) % nvec).wait_recv()

        with_c = gall_c[:, 0:refl].reshape(panel, panel)
        y_with_c = gall_c[:, refl : 2 * refl].reshape(panel, panel)
        correction = product_t(secular_ref[...], with_c) - product_t(coeff, y_with_c)
        out_ref[:, 0:panel] = product_t(out_ref[:, 0:panel] - correction, pinv_ref[...])

        @pl.loop(1, nvec)
        def _(k):
            vec_copy(gall_c, send_c, recv_c, k, v).wait_send()

    @pl.loop(1, nvec)
    def _(k):
        vec_copy(gall_y, send_g, recv_g, k, v).wait_send()

    @pl.loop(1, nrow)
    def _(k):
        row_copy(k).wait_send()

    @pl.loop(0, zn)
    def _(zz):
        block = zz * yn + y
        for sign in (-1, 1):
            passes = zz <= z if sign > 0 else zz >= z

            @pl.when(z_ok(sign) & passes)
            def _():
                z_copy(kbuf.at[block], block, sign).wait_send()

        @pl.loop(0, yn)
        def _(yy):
            other = zz * yn + yy
            for sign in (-1, 1):
                passes = yy <= y if sign > 0 else yy >= y

                @pl.when(y_ok(sign) & passes)
                def _():
                    y_copy(kbuf.at[other], other, sign).wait_send()


def per_device(
    nrow, nvec,
    old_vectors, panel_source, secular, reflectors, wy_factor, cholesky_panel, panel_inverse,
):
    panel = secular.shape[1]
    old_count, ncol = old_vectors.shape
    refl = reflectors.shape[0]
    yn = max(1, math.isqrt(nvec // 2))
    zn = nvec // yn
    slots = -(-(3 * (panel // nvec) // 2) // 8) * 8
    v = lax.axis_index("vec")
    r = lax.axis_index("row")
    owner = panel_source // old_count
    local = panel_source % old_count
    order = jnp.arange(panel, dtype=jnp.int32)
    before = (owner[:, None] == owner[None, :]) & (order[None, :] < order[:, None])
    earlier = jnp.sum(before.astype(jnp.int32), axis=1)
    slot_index = owner * slots + earlier
    mine = jnp.where(owner == v, earlier, -1)
    hit = mine[None, :] == jnp.arange(slots, dtype=jnp.int32)[:, None]
    source = jnp.sum(jnp.where(hit, local[None, :] + 1, 0), axis=1) - 1
    chooser = (source[:, None] == jnp.arange(old_count, dtype=jnp.int32)[None, :]).astype(
        jnp.float32
    )
    own = jnp.concatenate([product(chooser, old_vectors), reflectors], axis=0)
    below = r * ncol + jnp.arange(ncol, dtype=jnp.int32) >= panel
    masked = jnp.where(below[None, :], cholesky_panel, 0.0)
    rows = slots + refl
    vmem = pl.BlockSpec(memory_space=pltpu.VMEM)
    dma = pltpu.SemaphoreType.DMA
    return pl.pallas_call(
        functools.partial(kernel, nrow, zn, yn, slots),
        out_shape=jax.ShapeDtypeStruct((secular.shape[0], ncol), jnp.float32),
        in_specs=[vmem] * 6,
        out_specs=vmem,
        scratch_shapes=[
            pltpu.VMEM((nvec, rows, ncol), jnp.float32),
            pltpu.VMEM((3 * refl, panel), jnp.float32),
            pltpu.VMEM((nrow, 3 * refl, panel), jnp.float32),
            pltpu.VMEM((nvec, refl, panel), jnp.float32),
            pltpu.VMEM((nvec, 2 * refl, panel), jnp.float32),
            pltpu.VMEM((secular.shape[0], nvec * slots), jnp.float32),
            dma,
            dma((2, nvec)),
            dma((2, nvec)),
            dma((nvec,)),
            dma((nrow,)),
            dma((nrow,)),
            dma((nvec,)),
            dma((nvec,)),
            dma((nvec,)),
            dma((nvec,)),
        ],
        compiler_params=pltpu.CompilerParams(
            collective_id=0, has_side_effects=True, vmem_limit_bytes=48 * 1024 * 1024
        ),
    )(own, masked, slot_index[None, :], secular, wy_factor, panel_inverse)


def solution(mesh):
    in_specs = (P("vec", "row"), P(), P("vec", None), P("vec", "row"), P(), P("vec", "row"), P())
    return jax.shard_map(
        functools.partial(per_device, mesh.shape["row"], mesh.shape["vec"]),
        mesh=mesh,
        in_specs=in_specs,
        out_specs=P("vec", "row"),
        check_vma=False,
    )
```

```python
import functools
import math

import jax
import jax.numpy as jnp
from jax import lax
from jax.experimental import pallas as pl
from jax.experimental.pallas import tpu as pltpu
from jax.sharding import PartitionSpec as P

MESH = pl.DeviceIdType.MESH


def product(left, right):
    return jnp.dot(left, right, precision=lax.Precision.HIGHEST, preferred_element_type=jnp.float32)


def product_t(left, right):
    return lax.dot_general(
        left,
        right,
        (((1,), (1,)), ((), ())),
        precision=lax.Precision.HIGHEST,
        preferred_element_type=jnp.float32,
    )


def kernel(
    nrow, zn, yn, slots,
    own_ref, chol_ref, slot_ref, secular_ref, wy_ref, pinv_ref,
    out_ref,
    kbuf, gram, gram_y, rbuf, rbuf_y, gall, smap,
    own_sem, send_k, recv_k, send_r, recv_r, send_ry, recv_ry, send_g, recv_g,
):
    nvec = zn * yn
    rows, ncol = own_ref.shape
    refl = rows - slots
    panel = secular_ref.shape[1]
    r = lax.axis_index("row")
    v = lax.axis_index("vec")
    z = v // yn
    y = v % yn
    share = (zn * (yn - 1) - (zn - 1)) / max(1, 2 * (zn - 1) * (yn - 1))
    late = min(max(round(share * ncol / 128), 1) * 128, ncol - 128)
    early = ncol - late

    barrier = pltpu.get_barrier_semaphore()

    @pl.loop(1, nrow)
    def _(k):
        pl.semaphore_signal(barrier, inc=1, device_id=((r + k) % nrow, v), device_id_type=MESH)

    @pl.loop(1, nvec)
    def _(k):
        pl.semaphore_signal(barrier, inc=1, device_id=(r, (v + k) % nvec), device_id_type=MESH)

    pl.semaphore_wait(barrier, nrow - 1 + nvec - 1)

    def z_ok(sign):
        return (z + sign >= 0) & (z + sign < zn)

    def y_ok(sign):
        return (y + sign >= 0) & (y + sign < yn)

    def part_copy(phase, part, block, target, lane, own):
        low, size = ((0, slots), (slots, refl))[phase]
        start, width = ((0, early), (early, late))[part]
        index = (pl.ds(low, size), pl.ds(start, width))
        held = kbuf.at[(block,) + index]
        return pltpu.make_async_remote_copy(
            src_ref=own_ref.at[index] if own else held,
            dst_ref=held,
            send_sem=send_k.at[phase, part, lane, block],
            recv_sem=recv_k.at[phase, part, block],
            device_id=(r, target),
            device_id_type=MESH,
        )

    def z_copy(phase, part, block, sign, own=False):
        return part_copy(phase, part, block, v + sign * yn, (sign + 1) // 2, own)

    def y_copy(phase, part, block, sign, own=False):
        return part_copy(phase, part, block, v + sign, 2 + (sign + 1) // 2, own)

    def z_send(phase, part, block, sign, own=False):
        @pl.when(z_ok(sign))
        def _():
            z_copy(phase, part, block, sign, own).start()

    def y_send(phase, part, block, sign, own=False):
        @pl.when(y_ok(sign))
        def _():
            y_copy(phase, part, block, sign, own).start()

    def arrived(phase, part, block):
        part_copy(phase, part, block, v, 0, False).wait_recv()

    def send_own(phase):
        for sign in (-1, 1):
            y_send(phase, 1, v, sign, True)
            z_send(phase, 0, v, sign, True)
        for sign in (-1, 1):
            y_send(phase, 0, v, sign, True)
            z_send(phase, 1, v, sign, True)

    def relay_first(phase):
        @pl.loop(1, yn)
        def _(h):
            for side in (-1, 1):
                yy = y + side * h

                @pl.when((yy >= 0) & (yy < yn))
                def _():
                    block = z * yn + yy
                    arrived(phase, 1, block)
                    y_send(phase, 1, block, -side)
                    for sign in (-1, 1):
                        z_send(phase, 1, block, sign)

    def relay(phase, use, hook):
        @pl.loop(1, zn + 1)
        def _(d):
            for side in (-1, 1):
                zz = z + side * d

                @pl.when((zz >= 0) & (zz < zn))
                def _():
                    block = zz * yn + y
                    arrived(phase, 0, block)
                    z_send(phase, 0, block, -side)
                    for sign in (-1, 1):
                        y_send(phase, 0, block, sign)

            for side in (-1, 1):
                zz = z + side * d

                @pl.when((zz >= 0) & (zz < zn))
                def _():
                    @pl.loop(0, yn)
                    def _(yy):
                        arrived(phase, 1, zz * yn + yy)
                        z_send(phase, 1, zz * yn + yy, -side)

            for side in (-1, 1):
                zz = z + side * d

                @pl.when((zz >= 0) & (zz < zn))
                def _():
                    use(zz * yn + y)

            e = d - 1
            for side in (-1, 1):
                zz = z + side * e

                @pl.when((zz >= 0) & (zz < zn) & ((side < 0) | (e > 0)))
                def _():
                    @pl.loop(1, yn)
                    def _(h):
                        for sign in (-1, 1):
                            yy = y + sign * h

                            @pl.when((yy >= 0) & (yy < yn))
                            def _():
                                block = zz * yn + yy
                                arrived(phase, 0, block)
                                y_send(phase, 0, block, -sign)
                                use(block)

            hook(d)

    own_copy = pltpu.make_async_copy(own_ref, kbuf.at[v], own_sem)
    send_own(0)
    own_copy.start()
    gram[...] = jnp.zeros_like(gram)
    gram_y[...] = jnp.zeros_like(gram_y)
    row_iota = lax.broadcasted_iota(jnp.int32, (nvec * slots, panel), 0)
    every = jnp.where(row_iota == slot_ref[0:1, :], 1.0, 0.0).astype(jnp.float32)
    smap[...] = product_t(secular_ref[...], every)

    step = math.gcd(ncol, 768)

    def add_picked(block):
        def body(i, carry):
            with_y, with_c = carry
            cols = pl.ds(pl.multiple_of(i * step, step), step)
            picked = kbuf[block, 0:slots, cols]
            with_y = with_y + product_t(own_ref[slots:rows, cols], picked)
            with_c = with_c + product_t(chol_ref[:, cols], picked)
            return with_y, with_c

        zero = jnp.zeros((refl, slots), jnp.float32)
        with_y, with_c = lax.fori_loop(0, ncol // step, body, (zero, zero))
        slot_iota = lax.broadcasted_iota(jnp.int32, (slots, panel), 0) + block * slots
        chosen = jnp.where(slot_iota == slot_ref[0:1, :], 1.0, 0.0).astype(jnp.float32)
        gram[0:refl] += product(with_y, chosen)
        gram[refl : 2 * refl] += product(with_c, chosen)

    def add_reflectors(block):
        def body(i, carry):
            cols = pl.ds(pl.multiple_of(i * step, step), step)
            return carry + product_t(chol_ref[:, cols], kbuf[block, slots:rows, cols])

        y_with_c = lax.fori_loop(0, ncol // step, body, jnp.zeros((refl, refl), jnp.float32))
        lane = lax.broadcasted_iota(jnp.int32, (refl, panel), 1)
        sub = lax.broadcasted_iota(jnp.int32, (refl, panel), 0) + block * refl
        placed = jnp.where(lane == sub, 1.0, 0.0).astype(jnp.float32)
        gram_y[...] += product(y_with_c, placed)

    own_copy.wait()
    relay_first(0)
    add_picked(v)
    relay(0, add_picked, lambda d: None)

    def row_copy(k, slot):
        return pltpu.make_async_remote_copy(
            src_ref=gram,
            dst_ref=rbuf.at[slot],
            send_sem=send_r.at[k],
            recv_sem=recv_r.at[slot],
            device_id=((r + k) % nrow, v),
            device_id_type=MESH,
        )

    def row_y_copy(slot):
        return pltpu.make_async_remote_copy(
            src_ref=gram_y,
            dst_ref=rbuf_y.at[slot],
            send_sem=send_ry,
            recv_sem=recv_ry.at[slot],
            device_id=(0, v),
            device_id_type=MESH,
        )

    def vec_copy(kind, k, slot):
        return pltpu.make_async_remote_copy(
            src_ref=gall.at[kind, v],
            dst_ref=gall.at[kind, slot],
            send_sem=send_g.at[kind, k],
            recv_sem=recv_g.at[kind, slot],
            device_id=(r, (v + k) % nvec),
            device_id_type=MESH,
        )

    def vec_start(kind):
        @pl.loop(1, nvec)
        def _(k):
            vec_copy(kind, k, v).start()

    def vec_arrive(kind):
        @pl.loop(1, nvec)
        def _(k):
            vec_copy(kind, k, (v + k) % nvec).wait_recv()

    def vec_sent(kind):
        @pl.loop(1, nvec)
        def _(k):
            vec_copy(kind, k, v).wait_send()

    wide = math.gcd(ncol, 512)

    def merge(low, high):
        @pl.loop(low, high)
        def _(i):
            cols = pl.ds(pl.multiple_of(i * wide, wide), wide)
            picked = kbuf[:, 0:slots, cols].reshape(nvec * slots, wide)
            out_ref[:, cols] = product(smap[...], picked)

    half = (ncol // wide) // 2

    @pl.loop(1, nrow)
    def _(k):
        row_copy(k, r).start()

    send_own(1)
    rbuf[r] = gram[...]
    relay_first(1)
    add_reflectors(v)

    def hook(d):
        @pl.when(d == 1)
        def _():
            @pl.loop(1, nrow)
            def _(k):
                row_copy(k, (r + k) % nrow).wait_recv()

            total = rbuf[0]
            for k in range(1, nrow):
                total = total + rbuf[k]
            gall[0, v] = total[0:refl]
            gall[1, v] = total[refl : 2 * refl]
            vec_start(0)

            @pl.when(r == 0)
            def _():
                vec_start(1)

            merge(0, half)

        @pl.when(d == 2)
        def _():
            merge(half, ncol // wide)

    relay(1, add_reflectors, hook)

    @pl.when(r != 0)
    def _():
        row_y_copy(r).start()

    vec_arrive(0)
    inner = product_t(secular_ref[...], gall[0].reshape(panel, panel))
    coeff = product_t(inner, wy_ref[...])

    @pl.when(r == 0)
    def _():
        total = gram_y[...]
        for k in range(1, nrow):
            row_y_copy(k).wait_recv()
            total = total + rbuf_y[k]
        gall[2, v] = total
        vec_start(2)

    @pl.loop(0, ncol // wide)
    def _(i):
        cols = pl.ds(pl.multiple_of(i * wide, wide), wide)
        householder = kbuf[:, slots:rows, cols].reshape(panel, wide)
        out_ref[:, cols] = out_ref[:, cols] - product(coeff, householder)

    @pl.when(r == 0)
    def _():
        vec_arrive(1)
        partial = product_t(secular_ref[...], gall[1].reshape(panel, panel))
        vec_arrive(2)
        correction = partial - product_t(coeff, gall[2].reshape(panel, panel))
        out_ref[:, 0:panel] = product_t(out_ref[:, 0:panel] - correction, pinv_ref[...])
        vec_sent(1)
        vec_sent(2)

    @pl.when(r != 0)
    def _():
        row_y_copy(r).wait_send()

    vec_sent(0)

    @pl.loop(1, nrow)
    def _(k):
        row_copy(k, r).wait_send()

    for phase in (0, 1):

        @pl.loop(0, zn)
        def _(zz):
            @pl.loop(0, yn)
            def _(yy):
                block = zz * yn + yy
                for sign in (-1, 1):
                    z_pass = (zz <= z if sign > 0 else zz >= z) & z_ok(sign)
                    y_pass = (yy <= y if sign > 0 else yy >= y) & y_ok(sign)

                    @pl.when(z_pass)
                    def _():
                        z_copy(phase, 1, block, sign).wait_send()

                    @pl.when(z_pass & (yy == y))
                    def _():
                        z_copy(phase, 0, block, sign).wait_send()

                    @pl.when(y_pass)
                    def _():
                        y_copy(phase, 0, block, sign).wait_send()

                    @pl.when(y_pass & (zz == z))
                    def _():
                        y_copy(phase, 1, block, sign).wait_send()


def per_device(
    nrow, nvec,
    old_vectors, panel_source, secular, reflectors, wy_factor, cholesky_panel, panel_inverse,
):
    panel = secular.shape[1]
    old_count, ncol = old_vectors.shape
    refl = reflectors.shape[0]
    yn = max(1, math.isqrt(nvec // 2))
    zn = nvec // yn
    slots = -(-(3 * (panel // nvec) // 2) // 8) * 8
    v = lax.axis_index("vec")
    r = lax.axis_index("row")
    owner = panel_source // old_count
    local = panel_source % old_count
    order = jnp.arange(panel, dtype=jnp.int32)
    before = (owner[:, None] == owner[None, :]) & (order[None, :] < order[:, None])
    earlier = jnp.sum(before.astype(jnp.int32), axis=1)
    slot_index = owner * slots + earlier
    mine = jnp.where(owner == v, earlier, -1)
    hit = mine[None, :] == jnp.arange(slots, dtype=jnp.int32)[:, None]
    source = jnp.sum(jnp.where(hit, local[None, :] + 1, 0), axis=1) - 1
    chooser = (source[:, None] == jnp.arange(old_count, dtype=jnp.int32)[None, :]).astype(
        jnp.float32
    )
    own = jnp.concatenate([product(chooser, old_vectors), reflectors], axis=0)
    below = r * ncol + jnp.arange(ncol, dtype=jnp.int32) >= panel
    masked = jnp.where(below[None, :], cholesky_panel, 0.0)
    rows = slots + refl
    vmem = pl.BlockSpec(memory_space=pltpu.VMEM)
    dma = pltpu.SemaphoreType.DMA
    return pl.pallas_call(
        functools.partial(kernel, nrow, zn, yn, slots),
        out_shape=jax.ShapeDtypeStruct((secular.shape[0], ncol), jnp.float32),
        in_specs=[vmem] * 6,
        out_specs=vmem,
        scratch_shapes=[
            pltpu.VMEM((nvec, rows, ncol), jnp.float32),
            pltpu.VMEM((2 * refl, panel), jnp.float32),
            pltpu.VMEM((refl, panel), jnp.float32),
            pltpu.VMEM((nrow, 2 * refl, panel), jnp.float32),
            pltpu.VMEM((nrow, refl, panel), jnp.float32),
            pltpu.VMEM((3, nvec, refl, panel), jnp.float32),
            pltpu.VMEM((secular.shape[0], nvec * slots), jnp.float32),
            dma,
            dma((2, 2, 4, nvec)),
            dma((2, 2, nvec)),
            dma((nrow,)),
            dma((nrow,)),
            dma,
            dma((nrow,)),
            dma((3, nvec)),
            dma((3, nvec)),
        ],
        compiler_params=pltpu.CompilerParams(
            collective_id=0, has_side_effects=True, vmem_limit_bytes=48 * 1024 * 1024
        ),
    )(own, masked, slot_index[None, :], secular, wy_factor, panel_inverse)


def solution(mesh):
    in_specs = (P("vec", "row"), P(), P("vec", None), P("vec", "row"), P(), P("vec", "row"), P())
    return jax.shard_map(
        functools.partial(per_device, mesh.shape["row"], mesh.shape["vec"]),
        mesh=mesh,
        in_specs=in_specs,
        out_specs=P("vec", "row"),
        check_vma=False,
    )
```

```python
import functools
import math

import jax
import jax.numpy as jnp
from jax import lax
from jax.experimental import pallas as pl
from jax.experimental.pallas import tpu as pltpu
from jax.sharding import PartitionSpec as P

MESH = pl.DeviceIdType.MESH


def product(left, right):
    return jnp.dot(left, right, precision=lax.Precision.HIGHEST, preferred_element_type=jnp.float32)


def product_t(left, right):
    return lax.dot_general(
        left,
        right,
        (((1,), (1,)), ((), ())),
        precision=lax.Precision.HIGHEST,
        preferred_element_type=jnp.float32,
    )


def kernel(
    nrow, zn, yn, slots,
    own_ref, chol_ref, slot_ref, secular_ref, wy_ref, pinv_ref,
    out_ref,
    kbuf, gram, gram_y, rbuf, rbuf_y, gall, smap,
    own_sem, send_k, recv_k, send_r, recv_r, send_ry, recv_ry, send_g, recv_g,
):
    nvec = zn * yn
    rows, ncol = own_ref.shape
    refl = rows - slots
    panel = secular_ref.shape[1]
    r = lax.axis_index("row")
    v = lax.axis_index("vec")
    z = v // yn
    y = v % yn
    share = (zn * (yn - 1) - (zn - 1)) / max(1, 2 * (zn - 1) * (yn - 1))
    late = min(max(round(share * ncol / 128), 1) * 128, ncol - 128)
    early = ncol - late

    barrier = pltpu.get_barrier_semaphore()

    @pl.loop(1, nrow)
    def _(k):
        pl.semaphore_signal(barrier, inc=1, device_id=((r + k) % nrow, v), device_id_type=MESH)

    @pl.loop(1, nvec)
    def _(k):
        pl.semaphore_signal(barrier, inc=1, device_id=(r, (v + k) % nvec), device_id_type=MESH)

    pl.semaphore_wait(barrier, nrow - 1 + nvec - 1)

    def z_ok(sign):
        return (z + sign >= 0) & (z + sign < zn)

    def y_ok(sign):
        return (y + sign >= 0) & (y + sign < yn)

    def part_copy(phase, part, block, target, lane, own):
        low, size = ((0, slots), (slots, refl))[phase]
        start, width = ((0, early), (early, late))[part]
        index = (pl.ds(low, size), pl.ds(start, width))
        held = kbuf.at[(block,) + index]
        return pltpu.make_async_remote_copy(
            src_ref=own_ref.at[index] if own else held,
            dst_ref=held,
            send_sem=send_k.at[phase, part, lane, block],
            recv_sem=recv_k.at[phase, part, block],
            device_id=(r, target),
            device_id_type=MESH,
        )

    def z_copy(phase, part, block, sign, own=False):
        return part_copy(phase, part, block, v + sign * yn, (sign + 1) // 2, own)

    def y_copy(phase, part, block, sign, own=False):
        return part_copy(phase, part, block, v + sign, 2 + (sign + 1) // 2, own)

    def z_send(phase, part, block, sign, own=False):
        @pl.when(z_ok(sign))
        def _():
            z_copy(phase, part, block, sign, own).start()

    def y_send(phase, part, block, sign, own=False):
        @pl.when(y_ok(sign))
        def _():
            y_copy(phase, part, block, sign, own).start()

    def arrived(phase, part, block):
        part_copy(phase, part, block, v, 0, False).wait_recv()

    def send_own(phase):
        for sign in (-1, 1):
            y_send(phase, 1, v, sign, True)
            z_send(phase, 0, v, sign, True)
        for sign in (-1, 1):
            y_send(phase, 0, v, sign, True)
            z_send(phase, 1, v, sign, True)

    def relay_first(phase):
        @pl.loop(1, yn)
        def _(h):
            for side in (-1, 1):
                yy = y + side * h

                @pl.when((yy >= 0) & (yy < yn))
                def _():
                    block = z * yn + yy
                    arrived(phase, 1, block)
                    y_send(phase, 1, block, -side)
                    for sign in (-1, 1):
                        z_send(phase, 1, block, sign)

    def relay(phase, use, hook):
        @pl.loop(1, zn + 1)
        def _(d):
            for side in (-1, 1):
                zz = z + side * d

                @pl.when((zz >= 0) & (zz < zn))
                def _():
                    block = zz * yn + y
                    arrived(phase, 0, block)
                    z_send(phase, 0, block, -side)
                    for sign in (-1, 1):
                        y_send(phase, 0, block, sign)

            for side in (-1, 1):
                zz = z + side * d

                @pl.when((zz >= 0) & (zz < zn))
                def _():
                    @pl.loop(0, yn)
                    def _(yy):
                        arrived(phase, 1, zz * yn + yy)
                        z_send(phase, 1, zz * yn + yy, -side)

            for side in (-1, 1):
                zz = z + side * d

                @pl.when((zz >= 0) & (zz < zn))
                def _():
                    if use is not None:
                        use(zz * yn + y)

            e = d - 1
            for side in (-1, 1):
                zz = z + side * e

                @pl.when((zz >= 0) & (zz < zn) & ((side < 0) | (e > 0)))
                def _():
                    @pl.loop(1, yn)
                    def _(h):
                        for sign in (-1, 1):
                            yy = y + sign * h

                            @pl.when((yy >= 0) & (yy < yn))
                            def _():
                                block = zz * yn + yy
                                arrived(phase, 0, block)
                                y_send(phase, 0, block, -sign)
                                if use is not None:
                                    use(block)

            hook(d)

    own_copy = pltpu.make_async_copy(own_ref, kbuf.at[v], own_sem)
    send_own(0)
    own_copy.start()
    gram_y[...] = jnp.zeros_like(gram_y)
    row_iota = lax.broadcasted_iota(jnp.int32, (nvec * slots, panel), 0)
    every = jnp.where(row_iota == slot_ref[0:1, :], 1.0, 0.0).astype(jnp.float32)
    smap[...] = product_t(secular_ref[...], every)

    step = math.gcd(ncol, 1024)

    def gram_picked():
        def body(i, carry):
            cols = pl.ds(pl.multiple_of(i * step, step), step)
            picked = kbuf[:, 0:slots, cols].reshape(nvec * slots, step)
            both = jnp.concatenate([own_ref[slots:rows, cols], chol_ref[:, cols]], axis=0)
            return carry + product_t(both, picked)

        zero = jnp.zeros((2 * refl, nvec * slots), jnp.float32)
        sums = lax.fori_loop(0, ncol // step, body, zero)
        slot_iota = lax.broadcasted_iota(jnp.int32, (nvec * slots, panel), 0)
        chosen = jnp.where(slot_iota == slot_ref[0:1, :], 1.0, 0.0).astype(jnp.float32)
        gram[...] = product(sums, chosen)

    def place(sums, first):
        lane = lax.broadcasted_iota(jnp.int32, (sums.shape[1], panel), 1)
        sub = lax.broadcasted_iota(jnp.int32, (sums.shape[1], panel), 0) + first
        gram_y[...] += product(sums, jnp.where(lane == sub, 1.0, 0.0).astype(jnp.float32))

    def add_reflectors(block):
        place(product_t(chol_ref[...], kbuf[block, slots:rows, :]), block * refl)

    own_copy.wait()
    relay_first(0)
    relay(0, None, lambda d: None)
    send_own(1)
    gram_picked()

    def row_copy(k, slot):
        return pltpu.make_async_remote_copy(
            src_ref=gram,
            dst_ref=rbuf.at[slot],
            send_sem=send_r.at[k],
            recv_sem=recv_r.at[slot],
            device_id=((r + k) % nrow, v),
            device_id_type=MESH,
        )

    def row_y_copy(slot):
        return pltpu.make_async_remote_copy(
            src_ref=gram_y,
            dst_ref=rbuf_y.at[slot],
            send_sem=send_ry,
            recv_sem=recv_ry.at[slot],
            device_id=(0, v),
            device_id_type=MESH,
        )

    def vec_copy(kind, k, slot):
        return pltpu.make_async_remote_copy(
            src_ref=gall.at[kind, v],
            dst_ref=gall.at[kind, slot],
            send_sem=send_g.at[kind, k],
            recv_sem=recv_g.at[kind, slot],
            device_id=(r, (v + k) % nvec),
            device_id_type=MESH,
        )

    def vec_start(kind):
        @pl.loop(1, nvec)
        def _(k):
            vec_copy(kind, k, v).start()

    def vec_arrive(kind):
        @pl.loop(1, nvec)
        def _(k):
            vec_copy(kind, k, (v + k) % nvec).wait_recv()

    def vec_sent(kind):
        @pl.loop(1, nvec)
        def _(k):
            vec_copy(kind, k, v).wait_send()

    wide = math.gcd(ncol, 512)

    def merge(low, high):
        @pl.loop(low, high)
        def _(i):
            cols = pl.ds(pl.multiple_of(i * wide, wide), wide)
            picked = kbuf[:, 0:slots, cols].reshape(nvec * slots, wide)
            out_ref[:, cols] = product(smap[...], picked)

    half = (ncol // wide) // 2

    @pl.loop(1, nrow)
    def _(k):
        row_copy(k, r).start()

    rbuf[r] = gram[...]
    relay_first(1)
    add_reflectors(v)

    def hook(d):
        @pl.when(d == 1)
        def _():
            @pl.loop(1, nrow)
            def _(k):
                row_copy(k, (r + k) % nrow).wait_recv()

            total = rbuf[0]
            for k in range(1, nrow):
                total = total + rbuf[k]
            gall[0, v] = total[0:refl]
            gall[1, v] = total[refl : 2 * refl]
            vec_start(0)

            @pl.when(r == 0)
            def _():
                vec_start(1)

            merge(0, half)

        @pl.when(d == 2)
        def _():
            merge(half, ncol // wide)

    relay(1, add_reflectors, hook)

    @pl.when(r != 0)
    def _():
        row_y_copy(r).start()

    vec_arrive(0)
    inner = product_t(secular_ref[...], gall[0].reshape(panel, panel))
    coeff = product_t(inner, wy_ref[...])

    @pl.when(r == 0)
    def _():
        total = gram_y[...]
        for k in range(1, nrow):
            row_y_copy(k).wait_recv()
            total = total + rbuf_y[k]
        gall[2, v] = total
        vec_start(2)

    @pl.loop(0, ncol // wide)
    def _(i):
        cols = pl.ds(pl.multiple_of(i * wide, wide), wide)
        householder = kbuf[:, slots:rows, cols].reshape(panel, wide)
        out_ref[:, cols] = out_ref[:, cols] - product(coeff, householder)

    @pl.when(r == 0)
    def _():
        vec_arrive(1)
        partial = product_t(secular_ref[...], gall[1].reshape(panel, panel))
        vec_arrive(2)
        correction = partial - product_t(coeff, gall[2].reshape(panel, panel))
        out_ref[:, 0:panel] = product_t(out_ref[:, 0:panel] - correction, pinv_ref[...])
        vec_sent(1)
        vec_sent(2)

    @pl.when(r != 0)
    def _():
        row_y_copy(r).wait_send()

    vec_sent(0)

    @pl.loop(1, nrow)
    def _(k):
        row_copy(k, r).wait_send()

    for phase in (0, 1):

        @pl.loop(0, zn)
        def _(zz):
            @pl.loop(0, yn)
            def _(yy):
                block = zz * yn + yy
                for sign in (-1, 1):
                    z_pass = (zz <= z if sign > 0 else zz >= z) & z_ok(sign)
                    y_pass = (yy <= y if sign > 0 else yy >= y) & y_ok(sign)

                    @pl.when(z_pass)
                    def _():
                        z_copy(phase, 1, block, sign).wait_send()

                    @pl.when(z_pass & (yy == y))
                    def _():
                        z_copy(phase, 0, block, sign).wait_send()

                    @pl.when(y_pass)
                    def _():
                        y_copy(phase, 0, block, sign).wait_send()

                    @pl.when(y_pass & (zz == z))
                    def _():
                        y_copy(phase, 1, block, sign).wait_send()


def per_device(
    nrow, nvec,
    old_vectors, panel_source, secular, reflectors, wy_factor, cholesky_panel, panel_inverse,
):
    panel = secular.shape[1]
    old_count, ncol = old_vectors.shape
    refl = reflectors.shape[0]
    yn = max(1, math.isqrt(nvec // 2))
    zn = nvec // yn
    slots = -(-(3 * (panel // nvec) // 2) // 8) * 8
    v = lax.axis_index("vec")
    r = lax.axis_index("row")
    owner = panel_source // old_count
    local = panel_source % old_count
    order = jnp.arange(panel, dtype=jnp.int32)
    before = (owner[:, None] == owner[None, :]) & (order[None, :] < order[:, None])
    earlier = jnp.sum(before.astype(jnp.int32), axis=1)
    slot_index = owner * slots + earlier
    mine = jnp.where(owner == v, earlier, -1)
    hit = mine[None, :] == jnp.arange(slots, dtype=jnp.int32)[:, None]
    source = jnp.sum(jnp.where(hit, local[None, :] + 1, 0), axis=1) - 1
    chooser = (source[:, None] == jnp.arange(old_count, dtype=jnp.int32)[None, :]).astype(
        jnp.float32
    )
    own = jnp.concatenate([product(chooser, old_vectors), reflectors], axis=0)
    below = r * ncol + jnp.arange(ncol, dtype=jnp.int32) >= panel
    masked = jnp.where(below[None, :], cholesky_panel, 0.0)
    rows = slots + refl
    vmem = pl.BlockSpec(memory_space=pltpu.VMEM)
    dma = pltpu.SemaphoreType.DMA
    return pl.pallas_call(
        functools.partial(kernel, nrow, zn, yn, slots),
        out_shape=jax.ShapeDtypeStruct((secular.shape[0], ncol), jnp.float32),
        in_specs=[vmem] * 6,
        out_specs=vmem,
        scratch_shapes=[
            pltpu.VMEM((nvec, rows, ncol), jnp.float32),
            pltpu.VMEM((2 * refl, panel), jnp.float32),
            pltpu.VMEM((refl, panel), jnp.float32),
            pltpu.VMEM((nrow, 2 * refl, panel), jnp.float32),
            pltpu.VMEM((nrow, refl, panel), jnp.float32),
            pltpu.VMEM((3, nvec, refl, panel), jnp.float32),
            pltpu.VMEM((secular.shape[0], nvec * slots), jnp.float32),
            dma,
            dma((2, 2, 4, nvec)),
            dma((2, 2, nvec)),
            dma((nrow,)),
            dma((nrow,)),
            dma,
            dma((nrow,)),
            dma((3, nvec)),
            dma((3, nvec)),
        ],
        compiler_params=pltpu.CompilerParams(
            collective_id=0, has_side_effects=True, vmem_limit_bytes=48 * 1024 * 1024
        ),
    )(own, masked, slot_index[None, :], secular, wy_factor, panel_inverse)


def solution(mesh):
    in_specs = (P("vec", "row"), P(), P("vec", None), P("vec", "row"), P(), P("vec", "row"), P())
    return jax.shard_map(
        functools.partial(per_device, mesh.shape["row"], mesh.shape["vec"]),
        mesh=mesh,
        in_specs=in_specs,
        out_specs=P("vec", "row"),
        check_vma=False,
    )
```
